32 devices in a mesh: scene: 2 (over y), aper: 8 (over z, x), range: 2 (over core).
Axes of the slice: x: 2, y: 2, z: 4, core: 2. Of those that a mesh axis runs over, the one named last changes fastest.
Arguments:
- images: bfloat16 [16, 2, 512, 256], P(('scene', 'aper'), None, None, 'range'), parts along dimension 0, may hold values from -6 to 6
- interp_matrix: bfloat16 [1024, 512], replicated, may hold values from -0.25 to 0.25
- offsets: int32 [3, 2, 1024], replicated, may hold values from -28 to 28, as said below
- tap_index: int32 [3, 2, 1024], replicated, may hold values from 0 to 15
- tap_table: float32 [16, 8], replicated, may hold values from -1.5 to 1.5
- phase_base: float32 [3, 2, 1024], replicated, may hold values from -3.140625 to 3.140625
- phase_slope: float32 [3, 2, 1024], replicated, may hold values from -0.5 to 0.5
Outputs:
- merged: bfloat16 [16, 2, 512, 256], P(('scene', 'aper'), None, None, 'range'), parts along dimension 0
The draws below stay inside these ranges and needn't reach their ends.
There are 2 independent parts, one for each index of `scene`. The reference program is written for one: setup_inputs(seed, part) draws one part's arguments, and reference() takes and returns one part's arrays. A program takes and returns all parts, laid end to end along the dimension named above; an argument that names none is the same for every part. Nothing has to cross between parts.
Inputs may be any that keep to these rules, and one draw needn't show every extreme that they name: `offsets`: for every level and role both -28 and 28 occur.
All inputs are finite; a program needn't handle non-finite values.
Results may differ from the reference program's by a relative error of at most 0.0085.
Values may be sent and summed in bfloat16 or wider, within the bound.
A program may use at most 64 MiB of HBM per device.

```python
from functools import partial
import jax
import jax.numpy as jnp
from jax import lax

ANG = 512
LEVELS = 3
HALO = 32
MAXOFF = 28
NFRAC = 16
TAPS = 8
APERS = 8
RANGE = 256
PARENT = 1024


def draw_offsets(key, part):
    values = jax.random.randint(jax.random.fold_in(key, 17), (LEVELS, 2, PARENT), -MAXOFF, MAXOFF + 1, dtype=jnp.int32)
    values = values.at[:, :, 0].set(-MAXOFF)
    values = values.at[:, :, 1].set(MAXOFF)
    return values


def plant(values, rng, smallest, high):
    longest = values.shape.index(max(values.shape))
    spots = []
    for shift in (0, 1):
        where = [jax.random.randint(jax.random.fold_in(rng, axis), (), 0, length) for axis, length in enumerate(values.shape)]
        where[longest] = (where[longest] + shift) % values.shape[longest]
        spots.append(tuple(where))
    return values.at[spots[0]].set(smallest).at[spots[1]].set(high)


def levels(own_key, extent, pieces, low, high):
    def one(axis_at, parts):
        steps = jax.random.uniform(jax.random.fold_in(jax.random.fold_in(own_key, 6), axis_at), (parts,), jnp.float32, low / len(pieces), high / len(pieces))
        return jnp.repeat(jnp.exp(steps), extent[axis_at] // parts).reshape((-1,) + (1,) * (len(extent) - axis_at - 1))

    factor_of = one(*pieces[0])
    for cut in pieces[1:]:
        factor_of = factor_of * one(*cut)
    return factor_of


def scatter_about(stream_key, dims, deviation, bound, cuts=(), held_as=jnp.bfloat16):
    array = jax.random.normal(stream_key, dims, jnp.float32) * deviation
    if len(cuts) > 0:
        array = levels(stream_key, dims, cuts, -0.22, 0.18) * array
    return jnp.clip(array, min=-bound, max=bound).astype(held_as)


def setup_inputs(seed: int = 0, part: int = 0) -> dict:
    key_list = jax.random.split(jax.random.key(seed), 8)
    own_keys = jax.random.split(jax.random.fold_in(key_list[7], part), 8)
    images = scatter_about(own_keys[0], (APERS, 2, ANG, RANGE), 1.0, 6.0, ((0, 8), (3, 2)))
    interp_matrix = scatter_about(key_list[1], (PARENT, ANG), ANG ** -0.5, 0.25)
    offsets = draw_offsets(jax.random.fold_in(key_list[7], 71), part)
    tap_index = plant(jax.random.randint(key_list[3], (LEVELS, 2, PARENT), 0, NFRAC), jax.random.fold_in(key_list[3], 1), 0, NFRAC - 1).astype(jnp.int32)
    tap_table = scatter_about(key_list[4], (NFRAC, TAPS), 0.25, 1.5, (), jnp.float32)
    phase_base = jnp.clip(jax.random.uniform(key_list[5], (LEVELS, 2, PARENT), jnp.float32, -3.140625, 3.140625), -3.140625, 3.140625)
    phase_slope = jnp.clip(jax.random.uniform(key_list[6], (LEVELS, 2, PARENT), jnp.float32, -0.5, 0.5), -0.5, 0.5)
    return dict(images=images, interp_matrix=interp_matrix, offsets=offsets, tap_index=tap_index, tap_table=tap_table, phase_base=phase_base, phase_slope=phase_slope)


def shifted(inter, shift_rows, tap_rows, first_col, out_width):
    taps_count = tap_rows.shape[1]
    needed = out_width + taps_count - 1
    total_width = inter.shape[2]
    start_cols = (first_col - 3 + shift_rows).astype(jnp.int32)
    moved = inter
    for bit_number in range((total_width - needed).bit_length()):
        stride_len = 1 << bit_number
        rolled = jnp.concatenate([moved[:, :, stride_len:], jnp.zeros_like(moved[:, :, :stride_len])], axis=2)
        chosen_bits = ((start_cols >> bit_number) & 1) == 1
        moved = jnp.where(chosen_bits[None, :, None], rolled, moved)
    window = moved[:, :, :needed]
    summed = jnp.zeros(window.shape[:2] + (out_width,), jnp.float32)
    for tap_number in range(taps_count):
        summed = summed + tap_rows[None, :, tap_number, None] * window[:, :, tap_number:tap_number + out_width].astype(jnp.float32)
    return summed


def child_term(inter, merge_level, child_role, offsets, tap_index, tap_table, phase_base, phase_slope):
    padded = jnp.pad(inter, ((0, 0), (0, 0), (HALO, HALO)))
    onehot = (tap_index[merge_level, child_role][:, None] == jnp.arange(NFRAC, dtype=jnp.int32)[None, :]).astype(jnp.float32)
    tap_rows = jnp.dot(onehot, tap_table, precision=lax.Precision.HIGHEST, preferred_element_type=jnp.float32)
    summed = shifted(padded, offsets[merge_level, child_role], tap_rows, HALO, RANGE)
    positions = jnp.arange(RANGE).astype(jnp.float32)
    phase_angle = phase_base[merge_level, child_role][:, None] + phase_slope[merge_level, child_role][:, None] * positions[None, :]
    cosine = jnp.cos(phase_angle)
    sine_part = jnp.sin(phase_angle)
    real_part = summed[0]
    imag_part = summed[1]
    return jnp.stack([real_part * cosine - imag_part * sine_part, real_part * sine_part + imag_part * cosine])


def merge_pair(merge_level, interp_matrix, offsets, tap_index, tap_table, phase_base, phase_slope, children):
    summed = jnp.zeros((2, PARENT, RANGE), jnp.float32)
    for child_role in range(2):
        inter = jnp.einsum("pa,can->cpn", interp_matrix.astype(jnp.float32), children[child_role].astype(jnp.float32),
                           precision=lax.Precision.HIGHEST).astype(jnp.bfloat16)
        summed = summed + child_term(inter, merge_level, child_role, offsets, tap_index, tap_table, phase_base, phase_slope)
    parent = summed.astype(jnp.bfloat16)
    return jnp.stack([parent[:, :ANG], parent[:, ANG:]])


def reference(images, interp_matrix, offsets, tap_index, tap_table, phase_base, phase_slope):
    current = images
    for merge_level in range(LEVELS):
        lower = 2 ** merge_level
        upper = APERS // (2 * lower)
        grouped = current.reshape(upper, 2, lower, 2, ANG, RANGE)
        pairs = jnp.transpose(grouped, (0, 2, 1, 3, 4, 5)).reshape(upper * lower, 2, 2, ANG, RANGE)
        merged = lax.map(partial(merge_pair, merge_level, interp_matrix, offsets, tap_index, tap_table, phase_base, phase_slope), pairs)
        current = jnp.transpose(merged.reshape(upper, lower, 2, 2, ANG, RANGE), (0, 2, 1, 3, 4, 5)).reshape(APERS, 2, ANG, RANGE)
    return current
```

```python
import functools

import jax
import jax.numpy as jnp
from jax import lax
from jax.experimental import pallas as pl
from jax.experimental.pallas import tpu as pltpu
from jax.sharding import PartitionSpec as P

MESH = pl.DeviceIdType.MESH
LANES = 128
GROUP = 16
BLOCKS = 4
CHUNKS = 2
F32 = jnp.float32
BF16 = jnp.bfloat16


def sincos(angle):
    turns = jnp.floor(angle * 0.6366197723675814 + 0.5)
    rest = angle - turns * 1.5703125
    rest = rest - turns * 4.837512969970703125e-4
    rest = rest - turns * 7.54978995489188216e-8
    quadrant = turns.astype(jnp.int32)
    square = rest * rest
    sine = rest + rest * square * (
        -1.6666654611e-1 + square * (8.3321608736e-3 + square * -1.9515295891e-4)
    )
    cosine = (1.0 - 0.5 * square) + square * square * (
        4.166664568298827e-2 + square * (-1.388731625493765e-3 + square * 2.443315711809948e-5)
    )
    odd = (quadrant & 1) == 1
    swapped_sine = jnp.where(odd, cosine, sine)
    swapped_cosine = jnp.where(odd, sine, cosine)
    sine = jnp.where((quadrant & 2) == 2, -swapped_sine, swapped_sine)
    cosine = jnp.where(((quadrant + 1) & 2) == 2, -swapped_cosine, swapped_cosine)
    return sine, cosine


def kernel(
    levels,
    cores,
    images,
    matrix,
    offsets,
    tap_index,
    tap_table,
    phase_base,
    phase_slope,
    out,
    image,
    rows_of,
    params,
    outgoing,
    incoming,
    mine,
    waves,
    handed,
    local_sem,
    first_sem,
    inter_sem,
    merge_sem,
):
    angles = image.shape[2]
    width = image.shape[3]
    span = width // cores
    pieces = width // LANES
    share = angles // cores
    rows = share // BLOCKS
    chunk = share // CHUNKS
    taps = tap_table.shape[1]
    scene = lax.axis_index("scene")
    aper = lax.axis_index("aper")
    core = lax.axis_index("range")
    first_row = pl.multiple_of(core * share, share)
    halves = [lax.rem(aper // 2**level, 2) for level in range(levels)]
    partners = [aper + (1 - 2 * halves[level]) * 2**level for level in range(levels)]
    others = [lax.rem(core + step, cores) for step in range(1, cores)]

    barrier = pltpu.get_barrier_semaphore()
    for partner in partners:
        pl.semaphore_signal(barrier, inc=1, device_id=(scene, partner, core), device_id_type=MESH)
    for other in others:
        pl.semaphore_signal(barrier, inc=1, device_id=(scene, aper, other), device_id_type=MESH)

    own_columns = pl.ds(pl.multiple_of(core * span, span), span)
    local_copies = [
        pltpu.make_async_copy(
            images.at[0], image.at[0, :, :, own_columns], local_sem.at[0]
        )
    ]
    for half in range(2):
        local_copies.append(
            pltpu.make_async_copy(
                matrix.at[pl.ds(half * angles + first_row, share), :],
                rows_of.at[half],
                local_sem.at[1 + half],
            )
        )
    for copy in local_copies:
        copy.start()

    def build_params(level):
        picked = pl.ds(pl.multiple_of(halves[level] * angles + core * share, LANES), share)
        index = tap_index[level, :, picked]
        weights = [jnp.zeros(index.shape, F32) for _ in range(taps)]
        for entry in range(tap_table.shape[0]):
            hit = index == entry
            for tap in range(taps):
                weights[tap] = jnp.where(hit, tap_table[entry, tap], weights[tap])
        start = offsets[level, :, picked].astype(F32) - 3.0
        base = phase_base[level, :, picked]
        slope = phase_slope[level, :, picked]
        for role in range(2):
            lines = [line[role : role + 1] for line in weights + [start, base, slope]]
            lines.append(jnp.zeros((LANES - len(lines), share), F32))
            params[level, role] = jnp.concatenate(lines, axis=0).T

    def wave(level, role, where):
        table = params[level, role, where, :]
        base = table[:, taps + 1 : taps + 2]
        slope = table[:, taps + 2 : taps + 3]
        lane = lax.broadcasted_iota(jnp.int32, (GROUP, LANES), 1).astype(F32)
        return [sincos(base + slope * (lane + float(LANES * piece))) for piece in range(pieces)]

    def term(level, role, where, parts, trig):
        table = params[level, role, where, :]
        lane = lax.broadcasted_iota(jnp.int32, (GROUP, LANES), 1)
        place = lane + table[:, taps : taps + 1].astype(jnp.int32)
        before = place < 0
        after = place >= LANES
        source = place & (LANES - 1)
        weights = [
            jnp.broadcast_to(table[:, tap : tap + 1], (GROUP, LANES)) for tap in range(taps)
        ]
        zero = jnp.zeros((GROUP, LANES), F32)
        shifted = []
        for part in parts:
            turned = [zero]
            for piece in range(pieces):
                value = part[:, piece * LANES : (piece + 1) * LANES].astype(F32)
                turned.append(
                    jnp.take_along_axis(value, source, axis=1, mode="promise_in_bounds")
                )
            turned += [zero, zero]
            window = [
                jnp.where(before, turned[piece], jnp.where(after, turned[piece + 2], turned[piece + 1]))
                for piece in range(pieces + 1)
            ]
            sums = []
            for piece in range(pieces):
                total = weights[0] * window[piece]
                for tap in range(1, taps):
                    mixed = jnp.where(lane >= tap, window[piece], window[piece + 1])
                    total = total + weights[tap] * pltpu.roll(mixed, LANES - tap, 1)
                sums.append(total)
            shifted.append(sums)
        real, imag = [], []
        for piece in range(pieces):
            sine, cosine = trig[piece]
            real.append(shifted[0][piece] * cosine - shifted[1][piece] * sine)
            imag.append(shifted[0][piece] * sine + shifted[1][piece] * cosine)
        return real, imag

    build_params(0)
    pl.semaphore_wait(barrier, len(partners) + len(others))

    first_copies = []
    for position, other in enumerate(others):
        copy = pltpu.make_async_remote_copy(
            src_ref=images.at[0],
            dst_ref=image.at[0, :, :, own_columns],
            send_sem=first_sem.at[0, position],
            recv_sem=first_sem.at[1, position],
            device_id=(scene, aper, other),
            device_id_type=MESH,
        )
        copy.start()
        first_copies.append(copy)
    for copy in local_copies:
        copy.wait()
    for copy in first_copies:
        copy.wait()

    def block_rows(block):
        return pl.ds(pl.multiple_of(block * rows, rows), rows)

    def inter_copy(level, block):
        picked = block_rows(block)
        return pltpu.make_async_remote_copy(
            src_ref=outgoing.at[level, :, picked, :],
            dst_ref=incoming.at[level, :, picked, :],
            send_sem=inter_sem.at[0, level, block],
            recv_sem=inter_sem.at[1, level, block],
            device_id=(scene, partners[level], core),
            device_id_type=MESH,
        )

    def merge_copy(level, block, position):
        picked = pl.ds(pl.multiple_of(first_row + block * rows, rows), rows)
        if level + 1 < levels:
            source = image.at[level + 1, :, picked, :]
            target = source
        else:
            source = handed.at[position, :, block_rows(block), :]
            target = out.at[0, :, picked, :]
        return pltpu.make_async_remote_copy(
            src_ref=source,
            dst_ref=target,
            send_sem=merge_sem.at[0, level, position, block],
            recv_sem=merge_sem.at[1, level, position, block],
            device_id=(scene, aper, others[position]),
            device_id_type=MESH,
        )

    for level in range(levels):
        half = halves[level]
        for piece in range(CHUNKS):
            picked = pl.ds(piece * chunk, chunk)
            for part in range(2):
                outgoing[level, part, picked, :] = jnp.dot(
                    rows_of[1 - half, picked, :], image[level, part], preferred_element_type=F32
                ).astype(BF16)
            for block in range(piece * BLOCKS // CHUNKS, (piece + 1) * BLOCKS // CHUNKS):
                inter_copy(level, block).start()

        for part in range(2):
            mine[part] = jnp.dot(
                rows_of[half], image[level, part], preferred_element_type=F32
            )
        if level + 1 < levels:
            build_params(level + 1)

        @pl.loop(0, share // GROUP)
        def _(group):
            where = pl.ds(pl.multiple_of(group * GROUP, GROUP), GROUP)
            parts = [mine[part, where, :].astype(BF16) for part in range(2)]
            real, imag = term(level, half, where, parts, wave(level, half, where))
            trig = wave(level, 1 - half, where)
            for piece in range(pieces):
                columns = slice(piece * LANES, (piece + 1) * LANES)
                mine[0, where, columns] = real[piece]
                mine[1, where, columns] = imag[piece]
                waves[0, where, columns] = trig[piece][0]
                waves[1, where, columns] = trig[piece][1]

        @pl.loop(0, BLOCKS)
        def _(block):
            inter_copy(level, block).wait_recv()

            @pl.loop(0, rows // GROUP)
            def _(group):
                start = pl.multiple_of(block * rows + group * GROUP, GROUP)
                where = pl.ds(start, GROUP)
                target = pl.ds(pl.multiple_of(first_row + start, GROUP), GROUP)
                parts = [incoming[level, part, where, :] for part in range(2)]
                trig = []
                for piece in range(pieces):
                    columns = slice(piece * LANES, (piece + 1) * LANES)
                    trig.append((waves[0, where, columns], waves[1, where, columns]))
                sums = term(level, 1 - half, where, parts, trig)
                for part in range(2):
                    merged = [
                        (
                            mine[part, where, piece * LANES : (piece + 1) * LANES]
                            + sums[part][piece]
                        ).astype(BF16)
                        for piece in range(pieces)
                    ]
                    if level + 1 < levels:
                        for piece in range(pieces):
                            columns = slice(piece * LANES, (piece + 1) * LANES)
                            image[level + 1, part, target, columns] = merged[piece]
                    else:
                        per_core = pieces // cores
                        for slot in range(per_core):
                            columns = slice(slot * LANES, (slot + 1) * LANES)
                            for position, owner in enumerate([core] + others):
                                chosen = merged[slot].astype(F32)
                                for rank in range(1, cores):
                                    chosen = jnp.where(
                                        owner == rank,
                                        merged[rank * per_core + slot].astype(F32),
                                        chosen,
                                    )
                                if position == 0:
                                    out[0, part, target, columns] = chosen.astype(BF16)
                                else:
                                    handed[position - 1, part, where, columns] = chosen.astype(BF16)

            for position in range(len(others)):
                merge_copy(level, block, position).start()

        @pl.loop(0, BLOCKS)
        def _(block):
            for position in range(len(others)):
                copy = merge_copy(level, block, position)
                copy.wait_send()
                sender = lax.rem(core + cores - 1 - position, cores)
                picked = pl.ds(pl.multiple_of(sender * share + block * rows, rows), rows)
                landed = (
                    image.at[level + 1, :, picked, :]
                    if level + 1 < levels
                    else out.at[0, :, picked, :]
                )
                pltpu.make_async_remote_copy(
                    src_ref=landed,
                    dst_ref=landed,
                    send_sem=merge_sem.at[0, level, position, block],
                    recv_sem=merge_sem.at[1, level, position, block],
                    device_id=(scene, aper, sender),
                    device_id_type=MESH,
                ).wait_recv()

    for level in range(levels):

        @pl.loop(0, BLOCKS)
        def _(block):
            inter_copy(level, block).wait_send()


def body(images, interp_matrix, offsets, tap_index, tap_table, phase_base, phase_slope):
    cores = lax.axis_size("range")
    levels = offsets.shape[0]
    angles = images.shape[2]
    width = images.shape[3] * cores
    share = angles // cores
    vmem = pl.BlockSpec(memory_space=pltpu.VMEM)
    anywhere = pl.BlockSpec(memory_space=pl.ANY)
    return pl.pallas_call(
        functools.partial(kernel, levels, cores),
        out_shape=jax.ShapeDtypeStruct(images.shape, images.dtype),
        in_specs=[
            anywhere,
            anywhere,
            vmem,
            vmem,
            pl.BlockSpec(memory_space=pltpu.SMEM),
            vmem,
            vmem,
        ],
        out_specs=vmem,
        scratch_shapes=[
            pltpu.VMEM((levels, 2, angles, width), BF16),
            pltpu.VMEM((2, share, angles), BF16),
            pltpu.VMEM((levels, 2, share, LANES), F32),
            pltpu.VMEM((levels, 2, share, width), BF16),
            pltpu.VMEM((levels, 2, share, width), BF16),
            pltpu.VMEM((2, share, width), F32),
            pltpu.VMEM((2, share, width), F32),
            pltpu.VMEM((cores - 1, 2, share, images.shape[3]), BF16),
            pltpu.SemaphoreType.DMA((3,)),
            pltpu.SemaphoreType.DMA((2, cores - 1)),
            pltpu.SemaphoreType.DMA((2, levels, BLOCKS)),
            pltpu.SemaphoreType.DMA((2, levels, cores - 1, BLOCKS)),
        ],
        compiler_params=pltpu.CompilerParams(collective_id=0, has_side_effects=True),
    )(images, interp_matrix, offsets, tap_index, tap_table, phase_base, phase_slope)


def solution(mesh):
    return jax.shard_map(
        body,
        mesh=mesh,
        in_specs=(P(("scene", "aper"), None, None, "range"), P(), P(), P(), P(), P(), P()),
        out_specs=P(("scene", "aper"), None, None, "range"),
        check_vma=False,
    )
```

```python
import functools

import jax
import jax.numpy as jnp
from jax import lax
from jax.experimental import pallas as pl
from jax.experimental.pallas import tpu as pltpu
from jax.sharding import PartitionSpec as P

MESH = pl.DeviceIdType.MESH
LANES = 128
REACH = 32
FINE = 8
SEND_LAG = 2
MERGE_LAG = 7
F32 = jnp.float32
BF16 = jnp.bfloat16


def sincos(angle):
    turns = jnp.floor(angle * 0.6366197723675814 + 0.5)
    rest = angle - turns * 1.5703125
    rest = rest - turns * 4.837512969970703125e-4
    rest = rest - turns * 7.54978995489188216e-8
    quadrant = turns.astype(jnp.int32)
    square = rest * rest
    sine = rest + rest * square * (
        -1.6666654611e-1 + square * (8.3321608736e-3 + square * -1.9515295891e-4)
    )
    cosine = (1.0 - 0.5 * square) + square * square * (
        4.166664568298827e-2 + square * (-1.388731625493765e-3 + square * 2.443315711809948e-5)
    )
    odd = (quadrant & 1) == 1
    swapped_sine = jnp.where(odd, cosine, sine)
    swapped_cosine = jnp.where(odd, sine, cosine)
    sine = jnp.where((quadrant & 2) == 2, -swapped_sine, swapped_sine)
    cosine = jnp.where(((quadrant + 1) & 2) == 2, -swapped_cosine, swapped_cosine)
    return sine, cosine


def kernel(
    levels,
    images,
    matrix,
    offsets,
    tap_index,
    tap_table,
    phase_base,
    phase_slope,
    out,
    image,
    rows_of,
    params,
    outgoing,
    incoming,
    kept,
    windows,
    merged,
    handed,
    local_sem,
    first_sem,
    inter_sem,
    merge_sem,
    last_sem,
):
    width = image.shape[2]
    angles = image.shape[3]
    span = images.shape[3]
    share = rows_of.shape[1]
    tiles = share // LANES
    steps = width // REACH
    per_owner = span // REACH
    taps = tap_table.shape[0]
    scene = lax.axis_index("scene")
    aper = lax.axis_index("aper")
    core = lax.axis_index("range")
    other = 1 - core
    first_row = pl.multiple_of(core * share, share)
    other_row = pl.multiple_of(other * share, share)
    halves = [lax.rem(aper // 2**level, 2) for level in range(levels)]
    partners = [aper + (1 - 2 * halves[level]) * 2**level for level in range(levels)]

    barrier = pltpu.get_barrier_semaphore()
    for partner in partners:
        pl.semaphore_signal(barrier, inc=1, device_id=(scene, partner, core), device_id_type=MESH)
    pl.semaphore_signal(barrier, inc=1, device_id=(scene, aper, other), device_id_type=MESH)

    local_copies = [
        pltpu.make_async_copy(
            matrix.at[pl.ds(half * angles + first_row, share), :],
            rows_of.at[half],
            local_sem.at[half],
        )
        for half in range(2)
    ]
    for copy in local_copies:
        copy.start()

    own_range = pl.ds(pl.multiple_of(core * span, span), span)
    for part in range(2):
        image[0, part, own_range, :] = images[0, part].T

    for level in range(levels):
        picked = pl.ds(pl.multiple_of(halves[level] * angles + core * share, LANES), share)
        index = tap_index[level, :, picked]
        weights = [jnp.zeros(index.shape, F32) for _ in range(taps)]
        for entry in range(tap_table.shape[1]):
            hit = index == entry
            for tap in range(taps):
                weights[tap] = jnp.where(hit, tap_table[tap, entry], weights[tap])
        lines = weights + [
            offsets[level, :, picked].astype(F32) + float(REACH - 3),
            phase_base[level, :, picked],
            phase_slope[level, :, picked],
        ]
        for row, line in enumerate(lines):
            for slot in range(2):
                role = halves[level] if slot == 0 else 1 - halves[level]
                params[level, slot, row : row + 1, :] = jnp.where(
                    role == 0, line[0:1], line[1:2]
                )
        edge = jnp.zeros((2, REACH, share), BF16)
        for buffer in (incoming, kept):
            buffer[level, :, 0:REACH, :] = edge
            buffer[level, :, REACH + width : REACH + width + REACH, :] = edge

    pl.semaphore_wait(barrier, len(partners) + 1)

    def first_copy(place):
        return pltpu.make_async_remote_copy(
            src_ref=image.at[0, :, place, :],
            dst_ref=image.at[0, :, place, :],
            send_sem=first_sem.at[0],
            recv_sem=first_sem.at[1],
            device_id=(scene, aper, other),
            device_id_type=MESH,
        )

    def inter_copy(level, step):
        return pltpu.make_async_remote_copy(
            src_ref=outgoing.at[level, :, pl.ds(pl.multiple_of(step * REACH, REACH), REACH), :],
            dst_ref=incoming.at[
                level, :, pl.ds(pl.multiple_of((step + 1) * REACH, REACH), REACH), :
            ],
            send_sem=inter_sem.at[0, level, step],
            recv_sem=inter_sem.at[1, level, step],
            device_id=(scene, partners[level], core),
            device_id_type=MESH,
        )

    def merge_copy(level, step, row):
        place = image.at[
            level, :, pl.ds(pl.multiple_of(step * REACH, REACH), REACH), pl.ds(row, share)
        ]
        return pltpu.make_async_remote_copy(
            src_ref=place,
            dst_ref=place,
            send_sem=merge_sem.at[0, level - 1, step],
            recv_sem=merge_sem.at[1, level - 1, step],
            device_id=(scene, aper, other),
            device_id_type=MESH,
        )

    def last_copy(row):
        return pltpu.make_async_remote_copy(
            src_ref=handed,
            dst_ref=out.at[0, :, pl.ds(row, share), :],
            send_sem=last_sem.at[0],
            recv_sem=last_sem.at[1],
            device_id=(scene, aper, other),
            device_id_type=MESH,
        )

    def send(level, step):
        if level > 0:
            merge_copy(level, step, other_row).wait_recv()
        here = pl.ds(pl.multiple_of(step * REACH, REACH), REACH)
        there = pl.ds(pl.multiple_of((step + 1) * REACH, REACH), REACH)
        both = jnp.concatenate([image[level, part, here, :] for part in range(2)], axis=0)
        for slot in range(2):
            half = 1 - halves[level] if slot == 0 else halves[level]
            inter = lax.dot_general(
                both, rows_of[half], (((1,), (1,)), ((), ())), preferred_element_type=F32
            ).astype(BF16)
            for part in range(2):
                piece = inter[part * REACH : (part + 1) * REACH]
                if slot == 0:
                    outgoing[level, part, here, :] = piece
                else:
                    kept[level, part, there, :] = piece
            if slot == 0:
                inter_copy(level, step).start()

    def term(level, slot, step, tile):
        buffer = kept if slot == 0 else incoming
        columns = slice(tile * LANES, (tile + 1) * LANES)

        def line(row, count):
            return jnp.broadcast_to(params[level, slot, row : row + 1, columns], (count, LANES))

        amount = line(taps, 2 * REACH).astype(jnp.int32)
        weights = [line(tap, REACH) for tap in range(taps)]
        order = lax.broadcasted_iota(jnp.int32, (REACH, LANES), 0) + step * REACH
        sine, cosine = sincos(
            line(taps + 1, REACH) + line(taps + 2, REACH) * order.astype(F32)
        )
        shifted = []
        for part in range(2):
            value = buffer[
                level, part, pl.ds(pl.multiple_of(step * REACH, REACH), 3 * REACH), columns
            ].astype(F32)
            keep = 2 * REACH
            bit = REACH
            value = jnp.concatenate(
                [
                    jnp.where((amount & bit) == bit, value[bit:], value[:keep]),
                    value[keep : keep + FINE],
                ],
                axis=0,
            )
            while bit > FINE:
                bit //= 2
                keep = value.shape[0] - bit
                value = jnp.where((amount[:keep] & bit) == bit, value[bit:], value[:keep])
            while bit > 1:
                bit //= 2
                turned = pltpu.roll(value, value.shape[0] - bit, 0)
                value = jnp.where((amount[: value.shape[0]] & bit) == bit, turned, value)
            window = windows.at[tile, slot, part]
            window[...] = value
            total = weights[0] * value[:REACH]
            for tap in range(1, taps):
                total = total + weights[tap] * window[tap : tap + REACH, :]
            shifted.append(total)
        return (
            shifted[0] * cosine - shifted[1] * sine,
            shifted[0] * sine + shifted[1] * cosine,
        )

    def merge(level, step):
        @pl.when(step == 0)
        def _():
            inter_copy(level, 0).wait_recv()

        @pl.when(step + 1 < steps)
        def _():
            inter_copy(level, step + 1).wait_recv()

        here = pl.ds(pl.multiple_of(step * REACH, REACH), REACH)
        for tile in range(tiles):
            terms = [term(level, slot, step, tile) for slot in range(2)]
            for part in range(2):
                total = terms[0][part] + terms[1][part]
                if level + 1 < levels:
                    columns = pl.ds(pl.multiple_of(first_row + tile * LANES, LANES), LANES)
                    image[level + 1, part, here, columns] = total.astype(BF16)
                else:
                    merged[part, here, tile * LANES : (tile + 1) * LANES] = total
        if level + 1 < levels:
            merge_copy(level + 1, step, first_row).start()
        else:

            @pl.when(lax.rem(step, per_owner) == per_owner - 1)
            def _():
                owner = step // per_owner
                block = pl.ds(pl.multiple_of(owner * span, span), span)

                @pl.when(owner == core)
                def _():
                    for part in range(2):
                        out[0, part, pl.ds(first_row, share), :] = merged[part, block, :].T.astype(BF16)

                @pl.when(owner != core)
                def _():
                    for part in range(2):
                        handed[part] = merged[part, block, :].T.astype(BF16)
                    last_copy(first_row).start()

    first = first_copy(own_range)
    first.start()
    for copy in local_copies:
        copy.wait()
    first.wait_send()
    first_copy(pl.ds(pl.multiple_of(other * span, span), span)).wait_recv()

    @pl.loop(0, steps)
    def _(step):
        send(0, step)

    stages = [(merge, 0, 0)]
    lag = 0
    for level in range(1, levels):
        lag += SEND_LAG
        stages.append((send, level, lag))
        lag += MERGE_LAG - SEND_LAG
        stages.append((merge, level, lag))

    @pl.loop(0, steps + lag)
    def _(tick):
        for stage, level, late in stages:

            @pl.when((tick >= late) & (tick < late + steps))
            def _():
                stage(level, tick - late)

    @pl.loop(0, steps)
    def _(step):
        for level in range(levels):
            inter_copy(level, step).wait_send()
            if level > 0:
                merge_copy(level, step, first_row).wait_send()

    last = last_copy(first_row)
    last.wait_send()
    last_copy(other_row).wait_recv()


def body(images, interp_matrix, offsets, tap_index, tap_table, phase_base, phase_slope):
    cores = lax.axis_size("range")
    levels = offsets.shape[0]
    angles = images.shape[2]
    span = images.shape[3]
    width = span * cores
    share = angles // cores
    steps = width // REACH
    vmem = pl.BlockSpec(memory_space=pltpu.VMEM)
    anywhere = pl.BlockSpec(memory_space=pl.ANY)
    framed = width + 2 * REACH
    return pl.pallas_call(
        functools.partial(kernel, levels),
        out_shape=jax.ShapeDtypeStruct(images.shape, images.dtype),
        in_specs=[
            vmem,
            anywhere,
            vmem,
            vmem,
            pl.BlockSpec(memory_space=pltpu.SMEM),
            vmem,
            vmem,
        ],
        out_specs=vmem,
        scratch_shapes=[
            pltpu.VMEM((levels, 2, width, angles), BF16),
            pltpu.VMEM((2, share, angles), BF16),
            pltpu.VMEM((levels, 2, 16, share), F32),
            pltpu.VMEM((levels, 2, width, share), BF16),
            pltpu.VMEM((levels, 2, framed, share), BF16),
            pltpu.VMEM((levels, 2, framed, share), BF16),
            pltpu.VMEM((share // LANES, 2, 2, REACH + 2 * FINE, LANES), F32),
            pltpu.VMEM((2, width, share), F32),
            pltpu.VMEM((2, share, span), BF16),
            pltpu.SemaphoreType.DMA((2,)),
            pltpu.SemaphoreType.DMA((2,)),
            pltpu.SemaphoreType.DMA((2, levels, steps)),
            pltpu.SemaphoreType.DMA((2, levels - 1, steps)),
            pltpu.SemaphoreType.DMA((2,)),
        ],
        compiler_params=pltpu.CompilerParams(collective_id=0, has_side_effects=True),
    )(images, interp_matrix, offsets, tap_index, tap_table.T, phase_base, phase_slope)


def solution(mesh):
    return jax.shard_map(
        body,
        mesh=mesh,
        in_specs=(P(("scene", "aper"), None, None, "range"), P(), P(), P(), P(), P(), P()),
        out_specs=P(("scene", "aper"), None, None, "range"),
        check_vma=False,
    )
```

```python
import functools

import jax
import jax.numpy as jnp
from jax import lax
from jax.experimental import pallas as pl
from jax.experimental.pallas import tpu as pltpu
from jax.sharding import PartitionSpec as P

MESH = pl.DeviceIdType.MESH
LANES = 128
REACH = 32
FINE = 8
SEND_LAG = 1
MERGE_LAG = 5
F32 = jnp.float32
BF16 = jnp.bfloat16


def sincos(angle):
    turns = jnp.floor(angle * 0.6366197723675814 + 0.5)
    rest = angle - turns * 1.5703125
    rest = rest - turns * 4.837512969970703125e-4
    rest = rest - turns * 7.54978995489188216e-8
    quadrant = turns.astype(jnp.int32)
    square = rest * rest
    sine = rest + rest * square * (
        -1.6666654611e-1 + square * (8.3321608736e-3 + square * -1.9515295891e-4)
    )
    cosine = (1.0 - 0.5 * square) + square * square * (
        4.166664568298827e-2 + square * (-1.388731625493765e-3 + square * 2.443315711809948e-5)
    )
    odd = (quadrant & 1) == 1
    swapped_sine = jnp.where(odd, cosine, sine)
    swapped_cosine = jnp.where(odd, sine, cosine)
    sine = jnp.where((quadrant & 2) == 2, -swapped_sine, swapped_sine)
    cosine = jnp.where(((quadrant + 1) & 2) == 2, -swapped_cosine, swapped_cosine)
    return sine, cosine


def kernel(
    levels,
    images,
    matrix,
    offsets,
    tap_index,
    tap_table,
    phase_base,
    phase_slope,
    out,
    image,
    rows_of,
    params,
    outgoing,
    incoming,
    kept,
    windows,
    merged,
    handed,
    local_sem,
    first_sem,
    inter_sem,
    merge_sem,
    last_sem,
):
    width = image.shape[2]
    angles = image.shape[3]
    span = images.shape[3]
    share = rows_of.shape[1]
    tiles = share // LANES
    steps = width // REACH
    per_owner = span // REACH
    taps = tap_table.shape[0]
    scene = lax.axis_index("scene")
    aper = lax.axis_index("aper")
    core = lax.axis_index("range")
    other = 1 - core
    first_row = pl.multiple_of(core * share, share)
    other_row = pl.multiple_of(other * share, share)
    halves = [lax.rem(aper // 2**level, 2) for level in range(levels)]
    partners = [aper + (1 - 2 * halves[level]) * 2**level for level in range(levels)]

    barrier = pltpu.get_barrier_semaphore()
    for partner in partners:
        pl.semaphore_signal(barrier, inc=1, device_id=(scene, partner, core), device_id_type=MESH)
    pl.semaphore_signal(barrier, inc=1, device_id=(scene, aper, other), device_id_type=MESH)

    local_copies = [
        pltpu.make_async_copy(
            matrix.at[pl.ds(half * angles + first_row, share), :],
            rows_of.at[half],
            local_sem.at[half],
        )
        for half in range(2)
    ]
    for copy in local_copies:
        copy.start()

    own_range = pl.ds(pl.multiple_of(core * span, span), span)
    for part in range(2):
        image[0, part, own_range, :] = images[0, part].T

    for level in range(levels):
        picked = pl.ds(pl.multiple_of(halves[level] * angles + core * share, LANES), share)
        index = tap_index[level, :, picked]
        weights = [jnp.zeros(index.shape, F32) for _ in range(taps)]
        for entry in range(tap_table.shape[1]):
            hit = index == entry
            for tap in range(taps):
                weights[tap] = jnp.where(hit, tap_table[tap, entry], weights[tap])
        lines = weights + [
            offsets[level, :, picked].astype(F32) + float(REACH - 3),
            phase_base[level, :, picked],
            phase_slope[level, :, picked],
        ]
        for row, line in enumerate(lines):
            for slot in range(2):
                role = halves[level] if slot == 0 else 1 - halves[level]
                params[level, slot, row : row + 1, :] = jnp.where(
                    role == 0, line[0:1], line[1:2]
                )
        edge = jnp.zeros((2, REACH, share), BF16)
        for buffer in (incoming, kept):
            buffer[level, :, 0:REACH, :] = edge
            buffer[level, :, REACH + width : REACH + width + REACH, :] = edge

    pl.semaphore_wait(barrier, len(partners) + 1)

    def first_copy(place):
        return pltpu.make_async_remote_copy(
            src_ref=image.at[0, :, place, :],
            dst_ref=image.at[0, :, place, :],
            send_sem=first_sem.at[0],
            recv_sem=first_sem.at[1],
            device_id=(scene, aper, other),
            device_id_type=MESH,
        )

    def inter_copy(level, step):
        return pltpu.make_async_remote_copy(
            src_ref=outgoing.at[level, :, pl.ds(pl.multiple_of(step * REACH, REACH), REACH), :],
            dst_ref=incoming.at[
                level, :, pl.ds(pl.multiple_of((step + 1) * REACH, REACH), REACH), :
            ],
            send_sem=inter_sem.at[0, level, step],
            recv_sem=inter_sem.at[1, level, step],
            device_id=(scene, partners[level], core),
            device_id_type=MESH,
        )

    def merge_copy(level, step, row):
        place = image.at[
            level, :, pl.ds(pl.multiple_of(step * REACH, REACH), REACH), pl.ds(row, share)
        ]
        return pltpu.make_async_remote_copy(
            src_ref=place,
            dst_ref=place,
            send_sem=merge_sem.at[0, level - 1, step],
            recv_sem=merge_sem.at[1, level - 1, step],
            device_id=(scene, aper, other),
            device_id_type=MESH,
        )

    def last_copy(row):
        return pltpu.make_async_remote_copy(
            src_ref=handed,
            dst_ref=out.at[0, :, pl.ds(row, share), :],
            send_sem=last_sem.at[0],
            recv_sem=last_sem.at[1],
            device_id=(scene, aper, other),
            device_id_type=MESH,
        )

    def send(level, step):
        if level > 0:
            merge_copy(level, step, other_row).wait_recv()
        here = pl.ds(pl.multiple_of(step * REACH, REACH), REACH)
        there = pl.ds(pl.multiple_of((step + 1) * REACH, REACH), REACH)
        both = jnp.concatenate([image[level, part, here, :] for part in range(2)], axis=0)
        for slot in range(2):
            half = 1 - halves[level] if slot == 0 else halves[level]
            inter = lax.dot_general(
                both, rows_of[half], (((1,), (1,)), ((), ())), preferred_element_type=F32
            ).astype(BF16)
            for part in range(2):
                piece = inter[part * REACH : (part + 1) * REACH]
                if slot == 0:
                    outgoing[level, part, here, :] = piece
                else:
                    kept[level, part, there, :] = piece
            if slot == 0:
                inter_copy(level, step).start()

    def term(level, slot, step, tile):
        buffer = kept if slot == 0 else incoming
        columns = slice(tile * LANES, (tile + 1) * LANES)

        def line(row, count):
            return jnp.broadcast_to(params[level, slot, row : row + 1, columns], (count, LANES))

        amount = line(taps, 2 * REACH).astype(jnp.int32)
        weights = [line(tap, REACH) for tap in range(taps)]
        order = lax.broadcasted_iota(jnp.int32, (REACH, LANES), 0) + step * REACH
        sine, cosine = sincos(
            line(taps + 1, REACH) + line(taps + 2, REACH) * order.astype(F32)
        )
        shifted = []
        for part in range(2):
            value = buffer[
                level, part, pl.ds(pl.multiple_of(step * REACH, REACH), 3 * REACH), columns
            ].astype(F32)
            keep = 2 * REACH
            bit = REACH
            value = jnp.concatenate(
                [
                    jnp.where((amount & bit) == bit, value[bit:], value[:keep]),
                    value[keep : keep + FINE],
                ],
                axis=0,
            )
            while bit > FINE:
                bit //= 2
                keep = value.shape[0] - bit
                value = jnp.where((amount[:keep] & bit) == bit, value[bit:], value[:keep])
            while bit > 1:
                bit //= 2
                turned = pltpu.roll(value, value.shape[0] - bit, 0)
                value = jnp.where((amount[: value.shape[0]] & bit) == bit, turned, value)
            window = windows.at[tile, slot, part]
            window[...] = value
            total = weights[0] * value[:REACH]
            for tap in range(1, taps):
                total = total + weights[tap] * window[tap : tap + REACH, :]
            shifted.append(total)
        return (
            shifted[0] * cosine - shifted[1] * sine,
            shifted[0] * sine + shifted[1] * cosine,
        )

    def merge(level, step):
        @pl.when(step == 0)
        def _():
            inter_copy(level, 0).wait_recv()

        @pl.when(step + 1 < steps)
        def _():
            inter_copy(level, step + 1).wait_recv()

        here = pl.ds(pl.multiple_of(step * REACH, REACH), REACH)
        for tile in range(tiles):
            terms = [term(level, slot, step, tile) for slot in range(2)]
            for part in range(2):
                total = terms[0][part] + terms[1][part]
                if level + 1 < levels:
                    columns = pl.ds(pl.multiple_of(first_row + tile * LANES, LANES), LANES)
                    image[level + 1, part, here, columns] = total.astype(BF16)
                else:
                    merged[part, here, tile * LANES : (tile + 1) * LANES] = total
        if level + 1 < levels:
            merge_copy(level + 1, step, first_row).start()
        else:

            @pl.when(lax.rem(step, per_owner) == per_owner - 1)
            def _():
                owner = step // per_owner
                block = pl.ds(pl.multiple_of(owner * span, span), span)

                @pl.when(owner == core)
                def _():
                    for part in range(2):
                        out[0, part, pl.ds(first_row, share), :] = merged[part, block, :].T.astype(BF16)

                @pl.when(owner != core)
                def _():
                    for part in range(2):
                        handed[part] = merged[part, block, :].T.astype(BF16)
                    last_copy(first_row).start()

    first = first_copy(own_range)
    first.start()
    for copy in local_copies:
        copy.wait()
    first.wait_send()
    first_copy(pl.ds(pl.multiple_of(other * span, span), span)).wait_recv()

    @pl.loop(0, steps)
    def _(step):
        send(0, step)

    stages = [(merge, 0, 0)]
    lag = 0
    for level in range(1, levels):
        lag += SEND_LAG
        stages.append((send, level, lag))
        lag += MERGE_LAG - SEND_LAG
        stages.append((merge, level, lag))

    @pl.loop(0, steps + lag)
    def _(tick):
        for stage, level, late in stages:

            @pl.when((tick >= late) & (tick < late + steps))
            def _():
                stage(level, tick - late)

    @pl.loop(0, steps)
    def _(step):
        for level in range(levels):
            inter_copy(level, step).wait_send()
            if level > 0:
                merge_copy(level, step, first_row).wait_send()

    last = last_copy(first_row)
    last.wait_send()
    last_copy(other_row).wait_recv()


def body(images, interp_matrix, offsets, tap_index, tap_table, phase_base, phase_slope):
    cores = lax.axis_size("range")
    levels = offsets.shape[0]
    angles = images.shape[2]
    span = images.shape[3]
    width = span * cores
    share = angles // cores
    steps = width // REACH
    vmem = pl.BlockSpec(memory_space=pltpu.VMEM)
    anywhere = pl.BlockSpec(memory_space=pl.ANY)
    framed = width + 2 * REACH
    return pl.pallas_call(
        functools.partial(kernel, levels),
        out_shape=pltpu.VMEM(images.shape, images.dtype),
        in_specs=[
            vmem,
            anywhere,
            vmem,
            vmem,
            pl.BlockSpec(memory_space=pltpu.SMEM),
            vmem,
            vmem,
        ],
        out_specs=vmem,
        scratch_shapes=[
            pltpu.VMEM((levels, 2, width, angles), BF16),
            pltpu.VMEM((2, share, angles), BF16),
            pltpu.VMEM((levels, 2, 16, share), F32),
            pltpu.VMEM((levels, 2, width, share), BF16),
            pltpu.VMEM((levels, 2, framed, share), BF16),
            pltpu.VMEM((levels, 2, framed, share), BF16),
            pltpu.VMEM((share // LANES, 2, 2, REACH + 2 * FINE, LANES), F32),
            pltpu.VMEM((2, width, share), F32),
            pltpu.VMEM((2, share, span), BF16),
            pltpu.SemaphoreType.DMA((2,)),
            pltpu.SemaphoreType.DMA((2,)),
            pltpu.SemaphoreType.DMA((2, levels, steps)),
            pltpu.SemaphoreType.DMA((2, levels - 1, steps)),
            pltpu.SemaphoreType.DMA((2,)),
        ],
        compiler_params=pltpu.CompilerParams(collective_id=0, has_side_effects=True),
    )(images, interp_matrix, offsets, tap_index, tap_table.T, phase_base, phase_slope)


def solution(mesh):
    return jax.shard_map(
        body,
        mesh=mesh,
        in_specs=(P(("scene", "aper"), None, None, "range"), P(), P(), P(), P(), P(), P()),
        out_specs=P(("scene", "aper"), None, None, "range"),
        check_vma=False,
    )
```
